128 devices in a mesh: section: 4 (over x), expert: 32 (over z, y, core).
Axes of the slice: x: 4, y: 4, z: 4, core: 2. Of those that a mesh axis runs over, the one named last changes fastest.
Arguments:
- tokens: bfloat16 [4, 2, 2048, 7168], P('section', None, 'expert'), may hold values from -6 to 6
- expert_ids: int32 [4, 2, 2048, 2], P('section', None, 'expert'), may hold values from 0 to 7, all different within a row; in each aligned block of 64 rows (0 to 63, 64 to 127, ..., all dimensions but the last counted through in order) at most 20 rows name the same one
- gate_weights: float32 [4, 2, 2048, 2], P('section', None, 'expert'), may hold values from 0.1 to 1
- w_gate: bfloat16 [4, 32, 7168, 512], P('section', 'expert'), may hold values from -0.0625 to 0.0625
- w_up: bfloat16 [4, 32, 7168, 512], P('section', 'expert'), may hold values from -0.0625 to 0.0625
- w_down: bfloat16 [4, 32, 512, 7168], P('section', 'expert'), may hold values from -0.125 to 0.125
Outputs:
- passed: bfloat16 [4, 2, 2048, 7168], P('section', None, 'expert')
The draws below stay inside these ranges and needn't reach their ends.
Inputs may be any that keep to these rules, and one draw needn't show every extreme that they name: `expert_ids`: in each aligned block of 64 tokens of one micro-batch (the tokens of one device), the 2 experts of a token differ, and no expert is named by more than 20 tokens; some expert is named by exactly 20.
All inputs are finite; a program needn't handle non-finite values.
Results may differ from the reference program's by a relative error of at most 0.0045.
Values may be sent and summed in bfloat16 or wider, within the bound.
No kernel may reach another device: no remote copies, remote signals or barrier semaphores. Data moves between devices by JAX's collectives and lax.ppermute only.
A program may use at most 192 MiB of HBM per device.

```python
import math
import jax
import jax.numpy as jnp
import numpy as np
from jax import lax

D = 7168
FF = 2048
SPLIT = 4
TOP = 2
MB = 2
TOK_MB = 64
FF_DEV = 512
EXPERTS = 8
CAP = 20
TOKENS_S = 2048
N_SECTION = 4
N_EXPERT = 32


def levels(stream_key, extent, split, low, largest):
    level, own = 1.0, jax.random.fold_in(stream_key, 6)
    for position, shards_of in split:
        heights = jnp.exp(jax.random.uniform(jax.random.fold_in(own, position), (shards_of,), jnp.float32, low / len(split), largest / len(split)))
        level = level * jnp.repeat(heights, extent[position] // shards_of).reshape([-1 if axis == position else 1 for axis in range(len(extent))])
    return level


def routed_block(stream_key, own, number, rows, amount, top, bound, skew):
    order = jax.random.permutation(stream_key, amount)
    crowded, ordinary = shares(amount, rows * top, bound, skew, True), shares(amount, rows * top, bound, skew, False)
    places = jnp.arange(amount)

    def named(lengths, offset_by):
        used = int((lengths > 0).sum())
        fixed = max(1, used // 4)
        moved = fixed + (places - fixed + offset_by * (used - fixed)) % max(1, amount - fixed)
        return jnp.zeros((amount,), jnp.int32).at[order[jnp.where(places < fixed, places, moved)]].set(jnp.asarray(lengths, jnp.int32))

    lengths = jnp.where(number % 4 == 0, named(crowded, number // 4), named(ordinary, number - number // 4 - 1))
    mixed = jax.random.permutation(jax.random.fold_in(own, 3), amount)
    giver, receiver = mixed[0:amount // 2 * 2:2], mixed[1:amount // 2 * 2:2]
    room = jnp.minimum(lengths[giver] - 1, bound - lengths[receiver]) // 2
    room = jnp.where((giver == order[0]) | (receiver == order[0]) | (lengths[receiver] == 0), 0, jnp.maximum(room, 0))
    moved = jax.random.randint(jax.random.fold_in(own, 4), (amount // 2,), 0, 1 << 20) % (room + 1)
    lengths = lengths.at[giver].add(-moved).at[receiver].add(moved)
    items = jnp.searchsorted(jnp.cumsum(lengths), jnp.arange(rows * top), side="right").astype(jnp.int32)
    grid = items.reshape(top, rows).T
    grid = grid[jax.random.permutation(jax.random.fold_in(own, 1), rows)]
    offset_by = jax.random.randint(jax.random.fold_in(own, 2), (rows, 1), 0, top)
    return jnp.take_along_axis(grid, (jnp.arange(top)[None, :] + offset_by) % top, axis=1)


def shares(number_of, total, reach, skew, full):
    weights = [(1 << 20) // math.isqrt(standing ** skew) + 1 for standing in range(1, number_of + 1)]
    largest = reach if full else min(reach, max(-(-total // number_of), total * weights[0] // sum(weights)))
    least = 1 if total - largest >= number_of - 1 else 0
    given, rest = [largest] + [least] * (number_of - 1), total - largest - least * (number_of - 1)
    while rest > 0:
        free = [i for i in range(1, number_of) if given[i] < largest] or [i for i in range(1, number_of) if given[i] < reach]
        whole, budget = sum([weights[i] for i in free]), rest
        for i in free:
            extra = min(reach - given[i], max(1, budget * weights[i] // whole), rest)
            given[i] = given[i] + extra
            rest = rest - extra
    return np.array(given)


def centred(key, shape, spread, reach, pieces=(), held_as=jnp.bfloat16):
    factor_of = levels(key, shape, pieces, -0.22, 0.18) if pieces else 1.0
    entries = jax.random.normal(key, shape, jnp.float32) * spread * factor_of
    return jnp.minimum(jnp.maximum(entries, -reach), reach).astype(held_as)


def setup_inputs(seed: int = 0) -> dict:
    seeds = jax.random.split(jax.random.key(seed), 7)
    tokens = centred(seeds[0], (N_SECTION, MB, TOKENS_S, D), 1.0, 6.0, ((0, 4), (2, 32)))
    expert_ids_keys = jax.random.split(jax.random.fold_in(seeds[1], 1), N_SECTION * MB * TOKENS_S // TOK_MB)
    expert_ids_turns = jax.random.permutation(jax.random.fold_in(seeds[1], 3), N_SECTION * MB * TOKENS_S // TOK_MB)
    expert_ids = jax.vmap(lambda own, number: routed_block(jax.random.fold_in(seeds[1], 2), own, number, TOK_MB, EXPERTS, TOP, CAP, 2))(expert_ids_keys, expert_ids_turns).reshape((N_SECTION, MB, TOKENS_S, TOP))
    gate_weights = jnp.clip(0.1 + 0.9 * jax.random.uniform(seeds[2], (N_SECTION, MB, TOKENS_S, TOP), jnp.float32) ** levels(seeds[2], (N_SECTION, MB, TOKENS_S, TOP), ((0, 4), (2, 32)), -0.2, 0.2), 0.1, 1.0)
    w_gate = centred(seeds[3], (N_SECTION, N_EXPERT, D, FF_DEV), D ** -0.5, 0.0625, ((0, 4), (1, 32)))
    w_up = centred(seeds[4], (N_SECTION, N_EXPERT, D, FF_DEV), D ** -0.5, 0.0625, ((0, 4), (1, 32)))
    w_down = centred(seeds[5], (N_SECTION, N_EXPERT, FF_DEV, D), FF ** -0.5, 0.125, ((0, 4), (1, 32)))
    return {"tokens": tokens, "expert_ids": expert_ids, "gate_weights": gate_weights, "w_gate": w_gate, "w_up": w_up, "w_down": w_down}


def normalize(values):
    floats = values.astype(jnp.float32)
    inv_rms = lax.rsqrt(lax.optimization_barrier(jnp.mean(floats * floats, axis=-1, keepdims=True)) + 1e-06)
    return (floats * inv_rms).astype(jnp.bfloat16)

def slot_of(routes):
    flat_ids = routes.reshape(-1)
    onehot = (flat_ids[:, None] == jnp.arange(EXPERTS, dtype=jnp.int32)[None, :]).astype(jnp.int32)
    before = jnp.cumsum(onehot, axis=0) - onehot
    return lax.optimization_barrier(jnp.sum(before * onehot, axis=1)).astype(jnp.int32).reshape(routes.shape)

def expert_rows(operands):
    rows_in, gate_all, up_all, down_all = operands
    summed = jnp.zeros((rows_in.shape[0], D), jnp.float32)
    for shard_idx in range(SPLIT):
        gate_act = jnp.dot(rows_in, gate_all[shard_idx], preferred_element_type=jnp.float32)
        up_act = jnp.dot(rows_in, up_all[shard_idx], preferred_element_type=jnp.float32)
        hidden = (jax.nn.silu(gate_act) * up_act).astype(jnp.bfloat16)
        result = jnp.dot(hidden, down_all[shard_idx], preferred_element_type=jnp.float32).astype(jnp.bfloat16)
        summed = summed + result.astype(jnp.float32)
    return summed

def take_rows(block_rows, index_row):
    return block_rows[index_row]

def reference(tokens, expert_ids, gate_weights, w_gate, w_up, w_down):
    results = [None] * N_SECTION
    block_idx = jnp.broadcast_to(jnp.arange(N_EXPERT, dtype=jnp.int32)[:, None, None], (N_EXPERT, TOK_MB, TOP))
    token_idx = jnp.broadcast_to(jnp.arange(TOK_MB, dtype=jnp.int32)[None, :, None], (N_EXPERT, TOK_MB, TOP))
    for section_idx in range(N_SECTION):
        gate_section = w_gate[section_idx].reshape(EXPERTS, SPLIT, D, FF_DEV)
        up_section = w_up[section_idx].reshape(EXPERTS, SPLIT, D, FF_DEV)
        down_section = w_down[section_idx].reshape(EXPERTS, SPLIT, FF_DEV, D)
        section_out = []
        for micro_idx in range(MB):
            block_tok = tokens[section_idx, micro_idx].reshape(N_EXPERT, TOK_MB, D)
            routes = expert_ids[section_idx, micro_idx].reshape(N_EXPERT, TOK_MB, TOP)
            gate_vals = gate_weights[section_idx, micro_idx].reshape(N_EXPERT, TOK_MB, TOP)
            normed = normalize(block_tok)
            slot_idx = jax.vmap(slot_of)(routes)
            target = routes * CAP + slot_idx
            index_table = jnp.full((N_EXPERT, EXPERTS * CAP), TOK_MB, jnp.int32)
            index_table = index_table.at[block_idx, target].set(token_idx)
            padded = jnp.concatenate([normed, jnp.zeros((N_EXPERT, 1, D), jnp.bfloat16)], axis=1)
            gathered = jax.vmap(take_rows)(padded, index_table)
            gathered = gathered.reshape(N_EXPERT, EXPERTS, CAP, D).transpose(1, 0, 2, 3)
            gathered = gathered.reshape(EXPERTS, N_EXPERT * CAP, D)
            combined = lax.map(expert_rows, (gathered, gate_section, up_section, down_section))
            combined = combined.reshape(EXPERTS, N_EXPERT, CAP, D)
            picked = combined[routes, block_idx, slot_idx]
            mixed_out = block_tok.astype(jnp.float32) + lax.optimization_barrier(jnp.sum(gate_vals[..., None] * picked, axis=2))
            section_out.append(mixed_out.astype(jnp.bfloat16).reshape(TOKENS_S, D))
        results[(section_idx + 1) % N_SECTION] = jnp.stack(section_out, axis=0)
    return jnp.stack(results, axis=0)
```

```python
import jax
import jax.numpy as jnp
from jax import lax
from jax.sharding import PartitionSpec as P


SPLIT = 4
CORES = 2
SIDE = 4
NEAR = ((1, 0), (0, 1), (3, 0), (0, 3), (2, 0), (0, 2), (0, 0), (1, 1))
FAR = ((3, 3), (1, 3), (3, 1), (2, 1), (1, 2), (2, 3), (3, 2), (2, 2))
COLUMNS = ((0, 4608), (4608, 7168))


def normalize(values):
    floats = values.astype(jnp.float32)
    inv_rms = lax.rsqrt(jnp.mean(floats * floats, axis=-1, keepdims=True) + 1e-06)
    return (floats * inv_rms).astype(jnp.bfloat16)


def slots_of(routes):
    tok_rows = routes.shape[1]
    earlier = jnp.arange(tok_rows)[None, :] < jnp.arange(tok_rows)[:, None]
    same = routes[:, :, :, None, None] == routes[:, None, None, :, :]
    counted = jnp.where(earlier[None, :, None, :, None], same, False)
    return jnp.sum(counted.astype(jnp.int32), axis=(3, 4))


def matmul(a, b):
    return jnp.dot(a, b, preferred_element_type=jnp.float32)


def local(tokens, expert_ids, gate_weights, w_gate, w_up, w_down):
    n_dev = lax.axis_size("expert")
    n_chip = n_dev // CORES
    experts = n_dev // SPLIT
    share_chips = SPLIT // CORES
    rings = n_chip // SIDE
    micro_count, tok_rows, width = tokens.shape[1:]
    top_k = expert_ids.shape[-1]
    capacity = min(tok_rows, tok_rows * top_k * 5 // (4 * experts))
    rows_each = micro_count * capacity
    toks = micro_count * tok_rows
    local_tok = tokens[0].reshape(toks, width)
    gate_mat, up_mat, down_mat = w_gate[0, 0], w_up[0, 0], w_down[0, 0]

    siblings = [(i, i ^ 1) for i in range(n_dev)]
    n_section = lax.axis_size("section")
    ring = [(i, (i + 1) % n_section) for i in range(n_section)]

    def chip_at(chip, core, offset):
        sign = 1 - 2 * core
        up = (chip // SIDE + sign * offset[0] + rings) % rings
        along = (chip % SIDE + sign * offset[1] + SIDE) % SIDE
        return up * SIDE + along

    def hop(offset):
        return [
            (i, chip_at(i // CORES, i % CORES, offset) * CORES + i % CORES)
            for i in range(n_dev)
        ]

    def out_to(rows, offset):
        return rows if offset == (0, 0) else lax.ppermute(rows, "expert", hop(offset))

    def back_from(rows, offset):
        if offset == (0, 0):
            return rows
        return lax.ppermute(rows, "expert", [(b, a) for a, b in hop(offset)])

    def swap(rows):
        return lax.ppermute(rows, "expert", siblings)

    me = lax.axis_index("expert")
    routes = expert_ids[0]
    micro = jnp.arange(micro_count, dtype=jnp.int32)[:, None, None]
    target = routes * rows_each + micro * capacity + slots_of(routes)
    target = target.reshape(toks, top_k)
    weights = gate_weights[0].reshape(toks, top_k)
    normed = normalize(local_tok)

    def places(offset):
        expert = chip_at(me // CORES, me % CORES, offset) // share_chips
        return expert * rows_each + jnp.arange(rows_each, dtype=jnp.int32)

    def after(values, earlier):
        return lax.optimization_barrier((values, earlier))[0]

    def selected(offset, normed):
        match = places(offset)[:, None, None] == target[None, :, :]
        selector = jnp.sum(match.astype(jnp.int32), axis=2).astype(jnp.bfloat16)
        return matmul(selector, normed).astype(jnp.bfloat16)

    def mixer(offsets):
        spots = jnp.concatenate([places(offset) for offset in offsets])
        match = target[:, :, None] == spots[None, None, :]
        mix = jnp.sum(jnp.where(match, weights[:, :, None], jnp.float32(0.0)), axis=1)
        high = lax.reduce_precision(mix, 8, 7)
        low = lax.reduce_precision(mix - high, 8, 7)
        return jnp.concatenate([high, low], axis=0).astype(jnp.bfloat16)

    def mixed(mix, rows):
        both = matmul(mix, rows)
        return both[:toks] + both[toks:]

    def hidden_of(rows):
        gate_act = matmul(rows, gate_mat)
        up_act = matmul(rows, up_mat)
        return (jax.nn.silu(gate_act) * up_act).astype(jnp.bfloat16)

    def stage(offsets, arrived, columns):
        total = None
        crossed = [swap(rows) for rows in arrived]
        other = hidden_of(jnp.concatenate(crossed, axis=0))
        own = hidden_of(jnp.concatenate(arrived, axis=0))
        returned = []
        for first, last in columns:
            piece = down_mat[:, first:last]
            if total is not None:
                own, other = after((own, other), total)
            from_other = swap(matmul(other, piece).astype(jnp.bfloat16))
            total = matmul(own, piece) + from_other.astype(jnp.float32)
            total = total.astype(jnp.bfloat16)
            blocks = [
                back_from(total[k * rows_each : (k + 1) * rows_each], offset)
                for k, offset in enumerate(offsets)
            ]
            returned.append(blocks)
        return returned, total

    sent = [selected(offset, normed) for offset in NEAR]
    near = [out_to(rows, offset) for rows, offset in zip(sent, NEAR)]
    normed = after(normed, sent[-1])
    sent = [selected(offset, normed) for offset in FAR]
    far = [out_to(rows, offset) for rows, offset in zip(sent, FAR)]
    near_back, near_total = stage(NEAR, near, ((0, width),))
    far = after(far, near_total)
    far_back, far_total = stage(FAR, far, COLUMNS)
    mix = mixer(FAR)
    near_rows = jnp.concatenate(after(near_back[0], far_total), axis=0)
    total = local_tok.astype(jnp.float32) + mixed(mixer(NEAR), near_rows)
    passed = []
    out = total
    for (first, last), blocks in zip(COLUMNS, far_back):
        rows = jnp.concatenate(after(blocks, out), axis=0)
        out = (total[:, first:last] + mixed(mix, rows)).astype(jnp.bfloat16)
        passed.append(lax.ppermute(out, "section", ring))
    passed = jnp.concatenate(passed, axis=1)
    return passed.reshape(1, micro_count, tok_rows, width)


def solution(mesh):
    return jax.shard_map(
        local,
        mesh=mesh,
        in_specs=(
            P("section", None, "expert", None),
            P("section", None, "expert", None),
            P("section", None, "expert", None),
            P("section", "expert", None, None),
            P("section", "expert", None, None),
            P("section", "expert", None, None),
        ),
        out_specs=P("section", None, "expert", None),
        check_vma=False,
    )
```
